512 devices in a mesh: dp: 64 (over y, z), mp: 8 (over x, core).
Axes of the slice: x: 4, y: 8, z: 8, core: 2. Of those that a mesh axis runs over, the one named last changes fastest.
Arguments:
- hidden_state_rows: bfloat16 [32768, 8192], P('dp', 'mp'), may hold values from -6 to 6
- request_adapter_index: int32 [32768], P('dp'), may hold values from 0 to 63, as said below
- adapter_store_slot: int32 [64], replicated, may hold values from 0 to 63, as said below
- down_weight_store: bfloat16 [64, 4, 8192, 64], P('dp', None, 'mp'), may hold values from -0.0625 to 0.0625
- up_weight_store: bfloat16 [64, 4, 64, 8192], P('dp', None, None, 'mp'), may hold values from -0.75 to 0.75
Outputs:
- adapted_rows: bfloat16 [32768, 8192], P('dp', 'mp')
The draws below stay inside these ranges and needn't reach their ends.
Inputs may be any that keep to these rules, and one draw needn't show every extreme that they name: `request_adapter_index`: among the 512 requests of one index of dp no adapter is named more than 16 times; in every draw one adapter is named exactly 16 times by every index of dp. `adapter_store_slot`: each slot is used by exactly one adapter; slot s lies in store shard s.
All inputs are finite; a program needn't handle non-finite values.
Results may differ from the reference program's by a relative error of at most 0.0075.
Values may be sent and summed in bfloat16 or wider, within the bound.
A program may use at most 64 MiB of HBM per device.

```python
import jax
import jax.numpy as jnp
from jax import lax

MODEL_WIDTH = 8192
ADAPTER_RANK = 64
LAYER_COUNT = 4
ADP_DEV = 1
TOK_DEV = 512
ADAPTER_COUNT = 64
MOST = 16
TOKENS = 32768
N_DP = 64


def route_tables(key):
    slot_of = jax.random.permutation(jax.random.fold_in(key, 11), ADAPTER_COUNT).astype(jnp.int32)
    owner_hot = jax.random.randint(jax.random.fold_in(key, 12), (), 0, ADAPTER_COUNT // ADP_DEV)
    adapter_at = jnp.argsort(slot_of, stable=True).astype(jnp.int32)
    return (slot_of, owner_hot, adapter_at)


def draw_adapter_store_slot(key, part):
    return route_tables(key)[0]


def draw_request_adapter_index(key, part):
    slot_of, owner_hot, adapter_at = route_tables(key)
    rolled = jnp.roll(adapter_at, -(owner_hot * ADP_DEV))
    hot_ones = rolled[:ADP_DEV]
    others = rolled[ADP_DEV:]
    spare = TOK_DEV - ADP_DEV * MOST
    n_others = ADAPTER_COUNT - ADP_DEV

    def one_block(block):
        block_key = jax.random.fold_in(jax.random.fold_in(key, 100), block)
        mixed = others[jax.random.permutation(jax.random.fold_in(block_key, 1), n_others)]
        head = jnp.repeat(hot_ones, MOST)
        tail = mixed[jnp.arange(spare, dtype=jnp.int32) % n_others]
        whole = jnp.concatenate([head, tail])
        return whole[jax.random.permutation(jax.random.fold_in(block_key, 2), TOK_DEV)]
    blocks = jax.vmap(one_block)(jnp.arange(N_DP, dtype=jnp.int32))
    return blocks.reshape(TOKENS).astype(jnp.int32)


def shard_levels(stream_key, dims, pieces, smallest, high):
    loudness = 1.0
    for axis_at, parts in pieces:
        draws = jax.random.uniform(jax.random.fold_in(jax.random.fold_in(stream_key, 6), axis_at), (parts,), jnp.float32, smallest / len(pieces), high / len(pieces))
        loudness = loudness * jnp.repeat(jnp.exp(draws), dims[axis_at] // parts).reshape((-1,) + (1,) * (len(dims) - 1 - axis_at))
    return loudness


def noise(rng, dims, spread, most, shards=(), kind=jnp.bfloat16):
    values = jax.random.normal(rng, dims, jnp.float32) * spread
    if len(shards) > 0:
        values = shard_levels(rng, dims, shards, -0.22, 0.18) * values
    return jnp.clip(values, min=-most, max=most).astype(kind)


def setup_inputs(seed: int = 0) -> dict:
    keys = jax.random.split(jax.random.key(seed), 6)
    return {
        "hidden_state_rows": noise(keys[0], (TOKENS, MODEL_WIDTH), 1.0, 6.0, ((0, 64), (1, 8))),
        "request_adapter_index": draw_request_adapter_index(jax.random.fold_in(keys[5], 71), 0),
        "adapter_store_slot": draw_adapter_store_slot(jax.random.fold_in(keys[5], 71), 0),
        "down_weight_store": noise(keys[3], (ADAPTER_COUNT, LAYER_COUNT, MODEL_WIDTH, ADAPTER_RANK), MODEL_WIDTH ** -0.5, 0.0625, ((0, 64), (2, 8))),
        "up_weight_store": noise(keys[4], (ADAPTER_COUNT, LAYER_COUNT, ADAPTER_RANK, MODEL_WIDTH), ADAPTER_RANK ** -0.5, 0.75, ((0, 64), (3, 8))),
    }


epsilon = 1e-05

def adapter_layer(current, down_a, up_b):
    widened = current.astype(jnp.float32)
    mean_sq = lax.optimization_barrier(jnp.mean(widened * widened, axis=-1, keepdims=True))
    reduced = (jnp.dot(current, down_a, preferred_element_type=jnp.float32) * lax.rsqrt(mean_sq + epsilon)).astype(jnp.bfloat16)
    return (widened + jnp.dot(reduced, up_b, preferred_element_type=jnp.float32)).astype(jnp.bfloat16)

def reference(hidden_state_rows, request_adapter_index, adapter_store_slot, down_weight_store, up_weight_store):
    bucket = N_DP * MOST
    by_adapter = jnp.argsort(request_adapter_index, stable=True).astype(jnp.int32)
    counts = jax.ops.segment_sum(jnp.ones((TOKENS,), jnp.int32), request_adapter_index, ADAPTER_COUNT).astype(jnp.int32)
    starts = (jnp.cumsum(counts) - counts).astype(jnp.int32)

    def per_adapter(result, adapter):
        offsets = jnp.arange(bucket, dtype=jnp.int32)
        is_live = offsets < counts[adapter]
        picked = by_adapter[jnp.minimum(starts[adapter] + offsets, TOKENS - 1)]
        current = hidden_state_rows[picked]
        request_slot_index = adapter_store_slot[adapter]
        down_projected = lax.dynamic_index_in_dim(down_weight_store, request_slot_index, 0, keepdims=False)
        up_projected = lax.dynamic_index_in_dim(up_weight_store, request_slot_index, 0, keepdims=False)
        for layer_index in range(LAYER_COUNT):
            current = adapter_layer(current, down_projected[layer_index], up_projected[layer_index])
        placed = jnp.where(is_live, picked, TOKENS).astype(jnp.int32)
        return (result.at[placed].set(current, mode='drop'), None)
    result, _ = lax.scan(per_adapter, jnp.zeros((TOKENS, MODEL_WIDTH), jnp.bfloat16), jnp.arange(ADAPTER_COUNT, dtype=jnp.int32))
    return result
```

```python
import functools

import jax
import jax.numpy as jnp
from jax import lax
from jax.experimental import pallas as pl
from jax.experimental.pallas import tpu as pltpu
from jax.sharding import PartitionSpec as P

MESH = pl.DeviceIdType.MESH
F32 = jnp.float32
BF16 = jnp.bfloat16
EPSILON = 1e-05
MOST = 16
NT = (((1,), (1,)), ((), ()))


def near_first(n):
    order = []
    for step in range(1, n // 2 + 1):
        order.append(step)
        if n - step != step:
            order.append(n - step)
    return order


def chunks_of(nz):
    if nz == 8:
        return [[0, 4], [1, 5], [7, 3], [2, 6]]
    return [[dz] for dz in range(nz)]


class Group:
    def __init__(self, src_all, dst_all, send_sem, recv_sem):
        self.src_all, self.dst_all, self.send_sem, self.recv_sem = src_all, dst_all, send_sem, recv_sem

    def start(self, copies):
        for src, dst, device in copies:
            self.whole(src, dst, device).start()
        self.device = copies[0][2]

    def whole(self, src, dst, device):
        return pltpu.make_async_remote_copy(
            src_ref=src,
            dst_ref=dst,
            send_sem=self.send_sem,
            recv_sem=self.recv_sem,
            device_id=device,
            device_id_type=MESH,
        )

    def wait_recv(self):
        self.whole(self.dst_all, self.dst_all, self.device).wait_recv()

    def wait_send(self):
        self.whole(self.src_all, self.src_all, self.device).wait_send()


def kernel(
    ny,
    nz,
    nm,
    width,
    hidden_ref,
    target_row_ref,
    target_col_ref,
    down_ref,
    up_ref,
    out_ref,
    pa,
    pb,
    qa,
    qb,
    ra,
    rb,
    wa,
    wb,
    sa,
    sb,
    ta,
    tb,
    zs,
    rz,
    lw,
    gs,
    rg,
    ga,
    gf,
    dcat,
    acc,
    send_sem,
    recv_sem,
):
    chunks = chunks_of(nz)
    nc, nzc = len(chunks), len(chunks[0])
    layers, rank = down_ref.shape[0], down_ref.shape[2]
    cols = layers * rank
    half = hidden_ref.shape[1] // 2
    slots = nzc * ny * MOST
    me = lax.axis_index("dp")
    m = lax.axis_index("mp")
    y, z = lax.div(me, nz), lax.rem(me, nz)

    def at_y(d):
        return {"dp": lax.rem(y + d + ny, ny) * nz + z}

    def at_z(d):
        return {"dp": y * nz + lax.rem(z + d + nz, nz)}

    def at_m(d):
        return {"mp": lax.rem(m + d, nm)}

    y_order, z_order, m_order = near_first(ny), near_first(nz), near_first(nm)

    barrier = pltpu.get_barrier_semaphore()
    peers = [at_y(d) for d in y_order] + [at_z(d) for d in z_order] + [at_m(d) for d in m_order]
    for peer in peers:
        pl.semaphore_signal(barrier, inc=1, device_id=peer, device_id_type=MESH)

    groups = []

    def group(src_all, dst_all):
        made = Group(src_all, dst_all, send_sem.at[len(groups)], recv_sem.at[len(groups)])
        groups.append(made)
        return made

    def first_z(c):
        return 1 if chunks[c][0] == 0 else 0

    def y_copies(src, dst, c, sign):
        made = group(src.at[c, :, 1:ny], dst.at[c, :, 1:ny])
        made.start([(src.at[c, :, d], dst.at[c, :, d], at_y(sign * d)) for d in y_order])
        return made

    def z_copies(src, dst, c, sign):
        low = first_z(c)
        if low == nzc:
            return None
        made = group(src.at[c, low:nzc], dst.at[c, low:nzc])
        made.start(
            [(src.at[c, i], dst.at[c, i], at_z(sign * chunks[c][i])) for i in range(low, nzc)]
        )
        return made

    def received(made):
        if made is not None:
            made.wait_recv()

    def keep_y(src, dst, c):
        dst[c, :, 0] = src[c, :, 0]

    def keep_z(src, dst, c):
        if first_z(c):
            dst[c, 0] = src[c, 0]

    def pack(c):
        rows = lax.broadcasted_iota(jnp.int32, (slots, hidden_ref.shape[0]), 0) + c * slots
        pick = (rows == target_row_ref[...]).astype(F32).astype(BF16)
        packed = jnp.dot(pick, hidden_ref[...], preferred_element_type=F32).astype(BF16)
        pa[c] = packed[:, :half].reshape(nzc, ny, MOST, half)
        pb[c] = packed[:, half:].reshape(nzc, ny, MOST, half)

    def there_first(c):
        fa = y_copies(pa, qa, c, 1)
        fb = z_copies(pb, qb, c, 1)
        keep_y(pa, qa, c)
        keep_z(pb, qb, c)
        return fa, fb

    def there_second(c, first):
        fa, fb = first
        received(fa)
        second_a = z_copies(qa, ra, c, 1)
        received(fb)
        second_b = y_copies(qb, rb, c, 1)
        keep_z(qa, ra, c)
        keep_y(qb, rb, c)
        return second_a, second_b

    def rows_of(c, i):
        a = ra[c, i].reshape(ny * MOST, half)
        b = rb[c, i].reshape(ny * MOST, half)
        return jnp.concatenate([a, b], axis=1)

    def project(rows):
        down_part = jnp.dot(rows, dcat[...], preferred_element_type=F32)
        up_part = lax.dot_general(rows, up_ref[...], NT, preferred_element_type=F32)
        return down_part, up_part[:, : cols - rank]

    def share(parts, landing):
        made = group(landing.at[1:nm], landing.at[1:nm])
        made.start([(parts.at[lax.rem(m + d, nm)], landing.at[d], at_m(d)) for d in m_order])
        return made

    def spread(held):
        made = group(held.at[1:nm], held.at[1:nm])
        made.start([(held.at[0], held.at[d], at_m(d)) for d in m_order])
        return made

    def total_of(parts, landing):
        total = parts[m]
        for d in range(1, nm):
            total += landing[d]
        return total

    def partials(c, second):
        for made in second:
            received(made)
        for i in range(nzc):
            rows = rows_of(c, i)
            down_part, up_part = project(rows)
            wide = rows.astype(F32)
            square = jnp.sum(wide * wide, axis=1, keepdims=True)
            whole = jnp.concatenate(
                [down_part, up_part, jnp.broadcast_to(square, (rows.shape[0], rank))], axis=1
            )
            per = zs.shape[2]
            count = rows.shape[0] // per
            zs[c, i * count : (i + 1) * count] = whole.reshape(count, per, 2 * cols)
        return share(zs.at[c], rz.at[c])

    def solve(c, shared):
        shared.wait_recv()
        total = total_of(zs.at[c], rz.at[c])
        square = total[:, 2 * cols - 1 :]
        lows = []
        extra = jnp.zeros_like(total)
        for layer in range(layers):
            term = total[:, layer * rank : (layer + 1) * rank]
            mean = square
            if layer > 0:
                term = term + extra[:, layer * rank : (layer + 1) * rank]
                known = layer * rank
                lean = 2.0 * total[:, cols : cols + known] + extra[:, cols : cols + known]
                mean = square + jnp.sum(
                    jnp.concatenate(lows, axis=1) * lean, axis=1, keepdims=True
                )
            scale = lax.rsqrt(jnp.maximum(mean, 0.0) * (1.0 / width) + EPSILON)
            low = (term * scale).astype(BF16)
            lw[c, 0, :, layer * rank : (layer + 1) * rank] = low
            lows.append(low.astype(F32))
            if layer < layers - 1:
                extra = extra + jnp.dot(
                    lows[-1],
                    gf[layer * rank : (layer + 1) * rank],
                    preferred_element_type=F32,
                    precision=lax.Precision.HIGHEST,
                )
        return spread(lw.at[c])

    def finish(c, told):
        told.wait_recv()
        count = nm // nzc
        for i in range(nzc):
            low = jnp.concatenate(
                [lw[c, lax.rem(m - (i * count + j) + nm, nm)] for j in range(count)], axis=0
            )
            update = jnp.dot(low, up_ref[...], preferred_element_type=F32)
            done = (rows_of(c, i).astype(F32) + update).astype(BF16)
            wa[c, i] = done[:, :half].reshape(ny, MOST, half)
            wb[c, i] = done[:, half:].reshape(ny, MOST, half)
        back_a = z_copies(wa, sa, c, -1)
        back_b = y_copies(wb, sb, c, -1)
        keep_z(wa, sa, c)
        keep_y(wb, sb, c)
        return back_a, back_b

    def back_second(c, first):
        back_a, back_b = first
        received(back_a)
        second_a = y_copies(sa, ta, c, -1)
        received(back_b)
        second_b = z_copies(sb, tb, c, -1)
        keep_y(sa, ta, c)
        keep_z(sb, tb, c)
        return second_a, second_b

    def unpack(c, second):
        for made in second:
            received(made)
        lanes = lax.broadcasted_iota(jnp.int32, (hidden_ref.shape[0], slots), 1) + c * slots
        pick = (lanes == target_col_ref[...]).astype(F32).astype(BF16)
        for h, t in ((0, ta), (1, tb)):
            part = jnp.dot(pick, t[c].reshape(slots, half), preferred_element_type=F32)
            cut = slice(h * half, (h + 1) * half)
            if c > 0:
                part = part + acc[:, cut]
            if c < nc - 1:
                acc[:, cut] = part
            else:
                out_ref[:, cut] = part.astype(BF16)

    def gram_start():
        for layer in range(layers):
            dcat[:, layer * rank : (layer + 1) * rank] = down_ref[layer]
        down_part, up_part = project(up_ref[: cols - rank])
        whole = jnp.concatenate(
            [down_part, up_part, jnp.zeros((cols - rank, rank), F32)], axis=1
        )
        gs[...] = whole.reshape(gs.shape)
        return share(gs, rg)

    def gram_sum(shared):
        shared.wait_recv()
        ga[0] = total_of(gs, rg)
        return spread(ga)

    def gram_end(told):
        told.wait_recv()
        per = ga.shape[1]
        for j in range(nm):
            gf[j * per : (j + 1) * per] = ga[lax.rem(m - j + nm, nm)]

    first, second, shared, told, back, last = [{} for _ in range(6)]
    pack(0)
    pl.semaphore_wait(barrier, len(peers))
    first[0] = there_first(0)
    gram = gram_start()
    for c in range(1, nc):
        pack(c)
        first[c] = there_first(c)
        second[c - 1] = there_second(c - 1, first[c - 1])
    gram = gram_sum(gram)
    second[nc - 1] = there_second(nc - 1, first[nc - 1])
    shared[0] = partials(0, second[0])
    gram_end(gram)
    for step in range(1, nc + 3):
        if step < nc:
            shared[step] = partials(step, second[step])
        if 0 <= step - 1 < nc:
            told[step - 1] = solve(step - 1, shared[step - 1])
        if 0 <= step - 2 < nc:
            back[step - 2] = finish(step - 2, told[step - 2])
        if 0 <= step - 3 < nc:
            last[step - 3] = back_second(step - 3, back[step - 3])
    for c in range(nc):
        unpack(c, last[c])
    for made in groups:
        made.wait_send()


def grid_of(n):
    side = 1
    while side * side < n:
        side *= 2
    return n // side, side


def local(hidden_state_rows, request_adapter_index, adapter_store_slot, down_weight_store, up_weight_store):
    tokens, width_dev = hidden_state_rows.shape
    ny, nz = grid_of(lax.axis_size("dp"))
    nm = lax.axis_size("mp")
    adapters = adapter_store_slot.shape[0]
    _, layers, _, rank = down_weight_store.shape
    cols = layers * rank
    chunks = chunks_of(nz)
    nc, nzc = len(chunks), len(chunks[0])
    half = width_dev // 2

    adapter_ids = jnp.arange(adapters, dtype=jnp.int32)
    matches = request_adapter_index[:, None] == adapter_ids[None, :]
    owner = jnp.sum(jnp.where(matches, adapter_store_slot[None, :], 0), axis=1)
    request_ids = jnp.arange(tokens, dtype=jnp.int32)
    earlier = (request_adapter_index[:, None] == request_adapter_index[None, :]) & (
        request_ids[:, None] > request_ids[None, :]
    )
    position = jnp.sum(earlier.astype(jnp.int32), axis=1)
    me = lax.axis_index("dp")
    dy = (owner // nz - me // nz) % ny
    dz = (owner % nz - me % nz) % nz
    flat = [offset for chunk in chunks for offset in chunk]
    z_slot = sum(jnp.where(dz == offset, place, 0) for place, offset in enumerate(flat))
    target = (z_slot * ny + dy) * MOST + position

    blocks = pltpu.VMEM((nc, nzc, ny, MOST, half), BF16)
    per = nzc * ny * MOST // nm
    gram_rows = (cols - rank) // nm
    n_groups = 10 * nc + 2
    return pl.pallas_call(
        functools.partial(kernel, ny, nz, nm, width_dev * nm),
        out_shape=jax.ShapeDtypeStruct((tokens, width_dev), BF16),
        in_specs=[pl.BlockSpec(memory_space=pltpu.VMEM)] * 5,
        out_specs=pl.BlockSpec(memory_space=pltpu.VMEM),
        scratch_shapes=[blocks] * 12
        + [
            pltpu.VMEM((nc, nm, per, 2 * cols), F32),
            pltpu.VMEM((nc, nm, per, 2 * cols), F32),
            pltpu.VMEM((nc, nm, per, cols), BF16),
            pltpu.VMEM((nm, gram_rows, 2 * cols), F32),
            pltpu.VMEM((nm, gram_rows, 2 * cols), F32),
            pltpu.VMEM((nm, gram_rows, 2 * cols), F32),
            pltpu.VMEM((cols - rank, 2 * cols), F32),
            pltpu.VMEM((width_dev, cols), BF16),
            pltpu.VMEM((tokens, width_dev), F32),
            pltpu.SemaphoreType.DMA((n_groups,)),
            pltpu.SemaphoreType.DMA((n_groups,)),
        ],
        compiler_params=pltpu.CompilerParams(
            collective_id=0, has_side_effects=True, vmem_limit_bytes=60000 * 1024
        ),
    )(
        hidden_state_rows,
        target[None, :],
        target[:, None],
        down_weight_store[0],
        up_weight_store[0].reshape(cols, width_dev),
    )


def solution(mesh):
    return jax.shard_map(
        local,
        mesh=mesh,
        in_specs=(
            P("dp", "mp"),
            P("dp"),
            P(),
            P("dp", None, "mp", None),
            P("dp", None, None, "mp"),
        ),
        out_specs=P("dp", "mp"),
        check_vma=False,
    )
```

```python
import functools

import jax
import jax.numpy as jnp
from jax import lax
from jax.experimental import pallas as pl
from jax.experimental.pallas import tpu as pltpu
from jax.sharding import PartitionSpec as P

MESH = pl.DeviceIdType.MESH
F32 = jnp.float32
BF16 = jnp.bfloat16
EPSILON = 1e-05
MOST = 16
NT = (((1,), (1,)), ((), ()))


def near_first(n):
    order = []
    for step in range(1, n // 2 + 1):
        order.append(step)
        if n - step != step:
            order.append(n - step)
    return order


def chunks_of(nz):
    if nz == 8:
        return [[0, 4], [1, 5], [7, 3], [2, 6]]
    return [[dz] for dz in range(nz)]


class Group:
    def __init__(self, src_all, dst_all, send_sem, recv_sem):
        self.src_all, self.dst_all, self.send_sem, self.recv_sem = src_all, dst_all, send_sem, recv_sem

    def start(self, copies):
        for src, dst, device in copies:
            self.whole(src, dst, device).start()
        self.device = copies[0][2]

    def whole(self, src, dst, device):
        return pltpu.make_async_remote_copy(
            src_ref=src,
            dst_ref=dst,
            send_sem=self.send_sem,
            recv_sem=self.recv_sem,
            device_id=device,
            device_id_type=MESH,
        )

    def wait_recv(self):
        self.whole(self.dst_all, self.dst_all, self.device).wait_recv()

    def wait_send(self):
        self.whole(self.src_all, self.src_all, self.device).wait_send()


def kernel(
    ny,
    nz,
    nm,
    width,
    layers,
    index_ref,
    slot_ref,
    hidden_hbm,
    down_hbm,
    up_hbm,
    out_ref,
    hidden_ref,
    down_ref,
    up_ref,
    load_sem,
    pa,
    pb,
    qa,
    qb,
    ra,
    rb,
    wa,
    wb,
    sa,
    sb,
    ta,
    tb,
    zs,
    rz,
    lw,
    gs,
    rg,
    ga,
    gf,
    acc,
    send_sem,
    recv_sem,
):
    chunks = chunks_of(nz)
    nc, nzc = len(chunks), len(chunks[0])
    cols = down_ref.shape[0]
    rank = cols // layers
    tokens = hidden_ref.shape[0]
    half = hidden_ref.shape[1] // 2
    slots = nzc * ny * MOST
    me = lax.axis_index("dp")
    m = lax.axis_index("mp")
    y, z = lax.div(me, nz), lax.rem(me, nz)

    def at_y(d):
        return {"dp": lax.rem(y + d + ny, ny) * nz + z}

    def at_z(d):
        return {"dp": y * nz + lax.rem(z + d + nz, nz)}

    def at_m(d):
        return {"mp": lax.rem(m + d, nm)}

    y_order, z_order, m_order = near_first(ny), near_first(nz), near_first(nm)

    barrier = pltpu.get_barrier_semaphore()
    peers = [at_y(d) for d in y_order] + [at_z(d) for d in z_order] + [at_m(d) for d in m_order]
    for peer in peers:
        pl.semaphore_signal(barrier, inc=1, device_id=peer, device_id_type=MESH)

    loads = []
    for place, (src, dst) in enumerate(
        ((hidden_hbm, hidden_ref), (down_hbm, down_ref), (up_hbm, up_ref))
    ):
        load = pltpu.make_async_copy(src, dst, load_sem.at[place])
        load.start()
        loads.append(load)

    def iota(shape, axis):
        return lax.broadcasted_iota(jnp.int32, shape, axis)

    def turned(row):
        n = row.shape[1]
        same = iota((n, n), 0) == iota((n, n), 1)
        return jnp.sum(jnp.where(same, row, 0.0), axis=1, keepdims=True)

    def place_of(owner, position):
        owner = owner.astype(jnp.int32)
        dy = lax.rem(lax.div(owner, nz) - y + ny, ny)
        dz = lax.rem(lax.rem(owner, nz) - z + nz, nz)
        flat = [offset for chunk in chunks for offset in chunk]
        z_slot = sum(jnp.where(dz == offset, i, 0) for i, offset in enumerate(flat))
        return (z_slot * ny + dy) * MOST + position.astype(jnp.int32)

    index_row = index_ref[...].astype(F32)
    slot_row = slot_ref[...].astype(F32)
    index_col, slot_col = turned(index_row), turned(slot_row)
    adapters = slot_row.shape[1]
    same = index_col == index_row
    row_at, col_at = iota((tokens, tokens), 0), iota((tokens, tokens), 1)
    position_row = jnp.sum(jnp.where(same & (row_at < col_at), 1.0, 0.0), axis=0, keepdims=True)
    position_col = jnp.sum(jnp.where(same & (col_at < row_at), 1.0, 0.0), axis=1, keepdims=True)
    named = iota((adapters, tokens), 0).astype(F32) == index_row
    owner_row = jnp.sum(jnp.where(named, slot_col, 0.0), axis=0, keepdims=True)
    named = iota((tokens, adapters), 1).astype(F32) == index_col
    owner_col = jnp.sum(jnp.where(named, slot_row, 0.0), axis=1, keepdims=True)
    target_row = place_of(owner_row, position_row)
    target_col = place_of(owner_col, position_col)

    groups = []

    def group(src_all, dst_all):
        made = Group(src_all, dst_all, send_sem.at[len(groups)], recv_sem.at[len(groups)])
        groups.append(made)
        return made

    def first_z(c):
        return 1 if chunks[c][0] == 0 else 0

    def y_copies(src, dst, c, sign):
        made = group(src.at[c, :, 1:ny], dst.at[c, :, 1:ny])
        made.start([(src.at[c, :, d], dst.at[c, :, d], at_y(sign * d)) for d in y_order])
        return made

    def z_copies(src, dst, c, sign):
        low = first_z(c)
        if low == nzc:
            return None
        made = group(src.at[c, low:nzc], dst.at[c, low:nzc])
        made.start(
            [(src.at[c, i], dst.at[c, i], at_z(sign * chunks[c][i])) for i in range(low, nzc)]
        )
        return made

    def received(made):
        if made is not None:
            made.wait_recv()

    def keep_y(src, dst, c):
        dst[c, :, 0] = src[c, :, 0]

    def keep_z(src, dst, c):
        if first_z(c):
            dst[c, 0] = src[c, 0]

    def pack(c):
        rows = lax.broadcasted_iota(jnp.int32, (slots, hidden_ref.shape[0]), 0) + c * slots
        pick = (rows == target_row).astype(F32).astype(BF16)
        packed = jnp.dot(pick, hidden_ref[...], preferred_element_type=F32).astype(BF16)
        pa[c] = packed[:, :half].reshape(nzc, ny, MOST, half)
        pb[c] = packed[:, half:].reshape(nzc, ny, MOST, half)

    def there_first(c):
        fa = y_copies(pa, qa, c, 1)
        fb = z_copies(pb, qb, c, 1)
        keep_y(pa, qa, c)
        keep_z(pb, qb, c)
        return fa, fb

    def there_second(c, first):
        fa, fb = first
        received(fa)
        second_a = z_copies(qa, ra, c, 1)
        received(fb)
        second_b = y_copies(qb, rb, c, 1)
        keep_z(qa, ra, c)
        keep_y(qb, rb, c)
        return second_a, second_b

    def rows_of(c, i):
        a = ra[c, i].reshape(ny * MOST, half)
        b = rb[c, i].reshape(ny * MOST, half)
        return jnp.concatenate([a, b], axis=1)

    def project(rows):
        down_part = lax.dot_general(rows, down_ref[...], NT, preferred_element_type=F32)
        up_part = lax.dot_general(rows, up_ref[...], NT, preferred_element_type=F32)
        return down_part, up_part[:, : cols - rank]

    def share(parts, landing):
        made = group(landing.at[1:nm], landing.at[1:nm])
        made.start([(parts.at[lax.rem(m + d, nm)], landing.at[d], at_m(d)) for d in m_order])
        return made

    def spread(held):
        made = group(held.at[1:nm], held.at[1:nm])
        made.start([(held.at[0], held.at[d], at_m(d)) for d in m_order])
        return made

    def total_of(parts, landing):
        total = parts[m]
        for d in range(1, nm):
            total += landing[d]
        return total

    def partials(c, second):
        for made in second:
            received(made)
        for i in range(nzc):
            rows = rows_of(c, i)
            down_part, up_part = project(rows)
            wide = rows.astype(F32)
            square = jnp.sum(wide * wide, axis=1, keepdims=True)
            whole = jnp.concatenate(
                [down_part, up_part, jnp.broadcast_to(square, (rows.shape[0], rank))], axis=1
            )
            per = zs.shape[2]
            count = rows.shape[0] // per
            zs[c, i * count : (i + 1) * count] = whole.reshape(count, per, 2 * cols)
        return share(zs.at[c], rz.at[c])

    def solve(c, shared):
        shared.wait_recv()
        total = total_of(zs.at[c], rz.at[c])
        square = total[:, 2 * cols - 1 :]
        lows = []
        extra = jnp.zeros_like(total)
        for layer in range(layers):
            term = total[:, layer * rank : (layer + 1) * rank]
            mean = square
            if layer > 0:
                term = term + extra[:, layer * rank : (layer + 1) * rank]
                known = layer * rank
                lean = 2.0 * total[:, cols : cols + known] + extra[:, cols : cols + known]
                mean = square + jnp.sum(
                    jnp.concatenate(lows, axis=1) * lean, axis=1, keepdims=True
                )
            scale = lax.rsqrt(jnp.maximum(mean, 0.0) * (1.0 / width) + EPSILON)
            low = (term * scale).astype(BF16)
            lw[c, 0, :, layer * rank : (layer + 1) * rank] = low
            lows.append(low.astype(F32))
            if layer < layers - 1:
                extra = extra + jnp.dot(
                    lows[-1],
                    gf[layer * rank : (layer + 1) * rank],
                    preferred_element_type=F32,
                    precision=lax.Precision.HIGHEST,
                )
        return spread(lw.at[c])

    def finish(c, told):
        told.wait_recv()
        count = nm // nzc
        for i in range(nzc):
            low = jnp.concatenate(
                [lw[c, lax.rem(m - (i * count + j) + nm, nm)] for j in range(count)], axis=0
            )
            update = jnp.dot(low, up_ref[...], preferred_element_type=F32)
            done = (rows_of(c, i).astype(F32) + update).astype(BF16)
            wa[c, i] = done[:, :half].reshape(ny, MOST, half)
            wb[c, i] = done[:, half:].reshape(ny, MOST, half)
        back_a = z_copies(wa, sa, c, -1)
        back_b = y_copies(wb, sb, c, -1)
        keep_z(wa, sa, c)
        keep_y(wb, sb, c)
        return back_a, back_b

    def back_second(c, first):
        back_a, back_b = first
        received(back_a)
        second_a = y_copies(sa, ta, c, -1)
        received(back_b)
        second_b = z_copies(sb, tb, c, -1)
        keep_y(sa, ta, c)
        keep_z(sb, tb, c)
        return second_a, second_b

    def unpack(c, second):
        for made in second:
            received(made)
        lanes = lax.broadcasted_iota(jnp.int32, (hidden_ref.shape[0], slots), 1) + c * slots
        pick = (lanes == target_col).astype(F32).astype(BF16)
        for h, t in ((0, ta), (1, tb)):
            part = jnp.dot(pick, t[c].reshape(slots, half), preferred_element_type=F32)
            cut = slice(h * half, (h + 1) * half)
            if c > 0:
                part = part + acc[:, cut]
            if c < nc - 1:
                acc[:, cut] = part
            else:
                out_ref[:, cut] = part.astype(BF16)

    def gram_parts():
        down_part, up_part = project(up_ref[: cols - rank])
        whole = jnp.concatenate(
            [down_part, up_part, jnp.zeros((cols - rank, rank), F32)], axis=1
        )
        gs[...] = whole.reshape(gs.shape)

    def gram_sum(shared):
        shared.wait_recv()
        ga[0] = total_of(gs, rg)
        return spread(ga)

    def gram_end(told):
        told.wait_recv()
        per = ga.shape[1]
        for j in range(nm):
            gf[j * per : (j + 1) * per] = ga[lax.rem(m - j + nm, nm)]

    loads[0].wait()
    for c in range(nc):
        pack(c)
    loads[1].wait()
    loads[2].wait()
    gram_parts()
    pl.semaphore_wait(barrier, len(peers))

    first, second, shared, told, back, last, gram = [{} for _ in range(7)]

    def do_first(c):
        first[c] = there_first(c)

    def do_second(c):
        second[c] = there_second(c, first[c])
        if c + 2 < nc:
            do_first(c + 2)

    def do_gram_share(c):
        gram[0] = share(gs, rg)

    def do_gram_sum(c):
        gram[1] = gram_sum(gram[0])

    def do_gram_end(c):
        gram_end(gram[1])

    def do_partials(c):
        shared[c] = partials(c, second[c])

    def do_solve(c):
        told[c] = solve(c, shared[c])

    def do_finish(c):
        back[c] = finish(c, told[c])

    def do_back(c):
        last[c] = back_second(c, back[c])

    def do_unpack(c):
        unpack(c, last[c])

    plan = [(1.0, 0, do_gram_share), (11.0, 0, do_gram_sum), (18.0, 0, do_gram_end)]
    for do, times in (
        (do_first, (0.0, 0.5)),
        (do_second, (7.5, 13.0, 25.0, 36.0)),
        (do_partials, (19.0, 30.5, 42.0, 48.5)),
        (do_solve, (28.0, 39.5, 51.0, 58.0)),
        (do_finish, (34.0, 45.0, 57.0, 63.5)),
        (do_back, (44.0, 56.0, 67.0, 76.0)),
        (do_unpack, (60.0, 70.0, 82.0, 93.0)),
    ):
        plan += [(time, c, do) for c, time in enumerate(times[:nc])]
    for _, c, do in sorted(plan, key=lambda step: step[0]):
        do(c)
    for made in groups:
        made.wait_send()


def grid_of(n):
    side = 1
    while side * side < n:
        side *= 2
    return n // side, side


def local(hidden_state_rows, request_adapter_index, adapter_store_slot, down_weight_store, up_weight_store):
    tokens, width_dev = hidden_state_rows.shape
    ny, nz = grid_of(lax.axis_size("dp"))
    nm = lax.axis_size("mp")
    _, layers, _, rank = down_weight_store.shape
    cols = layers * rank
    chunks = chunks_of(nz)
    nc, nzc = len(chunks), len(chunks[0])
    half = width_dev // 2

    blocks = pltpu.VMEM((nc, nzc, ny, MOST, half), BF16)
    per = nzc * ny * MOST // nm
    gram_rows = (cols - rank) // nm
    n_groups = 10 * nc + 2
    return pl.pallas_call(
        functools.partial(kernel, ny, nz, nm, width_dev * nm, layers),
        out_shape=jax.ShapeDtypeStruct((tokens, width_dev), BF16),
        in_specs=[pl.BlockSpec(memory_space=pltpu.VMEM)] * 2
        + [pl.BlockSpec(memory_space=pl.ANY)] * 3,
        out_specs=pl.BlockSpec(memory_space=pltpu.VMEM),
        scratch_shapes=[
            pltpu.VMEM((tokens, width_dev), BF16),
            pltpu.VMEM((cols, width_dev), BF16),
            pltpu.VMEM((cols, width_dev), BF16),
            pltpu.SemaphoreType.DMA((3,)),
        ]
        + [blocks] * 12
        + [
            pltpu.VMEM((nc, nm, per, 2 * cols), F32),
            pltpu.VMEM((nc, nm, per, 2 * cols), F32),
            pltpu.VMEM((nc, nm, per, cols), BF16),
            pltpu.VMEM((nm, gram_rows, 2 * cols), F32),
            pltpu.VMEM((nm, gram_rows, 2 * cols), F32),
            pltpu.VMEM((nm, gram_rows, 2 * cols), F32),
            pltpu.VMEM((cols - rank, 2 * cols), F32),
            pltpu.VMEM((tokens, width_dev), F32),
            pltpu.SemaphoreType.DMA((n_groups,)),
            pltpu.SemaphoreType.DMA((n_groups,)),
        ],
        compiler_params=pltpu.CompilerParams(
            collective_id=0, has_side_effects=True, vmem_limit_bytes=60000 * 1024
        ),
    )(
        request_adapter_index[None, :],
        adapter_store_slot[None, :],
        hidden_state_rows,
        jnp.swapaxes(down_weight_store[0], 1, 2).reshape(cols, width_dev),
        up_weight_store[0].reshape(cols, width_dev),
    )


def solution(mesh):
    return jax.shard_map(
        local,
        mesh=mesh,
        in_specs=(
            P("dp", "mp"),
            P("dp"),
            P(),
            P("dp", None, "mp", None),
            P("dp", None, None, "mp"),
        ),
        out_specs=P("dp", "mp"),
        check_vma=False,
    )
```

```python
import functools

import jax
import jax.numpy as jnp
from jax import lax
from jax.experimental import pallas as pl
from jax.experimental.pallas import tpu as pltpu
from jax.sharding import PartitionSpec as P

MESH = pl.DeviceIdType.MESH
ORDER = (
    "F0 F1 x0 G0 "
    "F2 y0 G1 F3 "
    "z0 P0 G2 S0 "
    "P1 U0 G3 S1 "
    "P2 B0 U1 P3 "
    "S2 B1 U2 S3 "
    "O0 U3 B2 O1 "
    "B3 O2 O3"
)
F32 = jnp.float32
BF16 = jnp.bfloat16
EPSILON = 1e-05
MOST = 16
NT = (((1,), (1,)), ((), ()))


def far_first(n):
    order = []
    for step in range(n // 2, 0, -1):
        if n - step != step:
            order.append(n - step)
        order.append(step)
    return order


def chunks_of(nz):
    if nz == 8:
        return [[0, 4], [2, 6], [1, 7], [3, 5]]
    return [[dz] for dz in range(nz)]


class Group:
    def __init__(self, src_all, dst_all, send_sem, recv_sem):
        self.src_all, self.dst_all, self.send_sem, self.recv_sem = src_all, dst_all, send_sem, recv_sem

    def start(self, copies):
        for src, dst, device in copies:
            self.whole(src, dst, device).start()
        self.device = copies[0][2]

    def whole(self, src, dst, device):
        return pltpu.make_async_remote_copy(
            src_ref=src,
            dst_ref=dst,
            send_sem=self.send_sem,
            recv_sem=self.recv_sem,
            device_id=device,
            device_id_type=MESH,
        )

    def wait_recv(self):
        self.whole(self.dst_all, self.dst_all, self.device).wait_recv()

    def wait_send(self):
        self.whole(self.src_all, self.src_all, self.device).wait_send()


def kernel(
    ny,
    nz,
    nm,
    width,
    layers,
    index_ref,
    slot_ref,
    hidden_hbm,
    down_hbm,
    up_hbm,
    out_ref,
    hidden_ref,
    down_ref,
    up_ref,
    load_sem,
    pa,
    pb,
    qa,
    qb,
    ra,
    rb,
    wa,
    wb,
    sa,
    sb,
    ta,
    tb,
    zs,
    rz,
    lw,
    gs,
    rg,
    ga,
    gf,
    acc,
    send_sem,
    recv_sem,
):
    chunks = chunks_of(nz)
    nc, nzc = len(chunks), len(chunks[0])
    cols = down_ref.shape[0]
    rank = cols // layers
    tokens = hidden_ref.shape[0]
    half = hidden_ref.shape[1] // 2
    slots = nzc * ny * MOST
    me = lax.axis_index("dp")
    m = lax.axis_index("mp")
    y, z = lax.div(me, nz), lax.rem(me, nz)

    def at_y(d):
        return {"dp": lax.rem(y + d + ny, ny) * nz + z}

    def at_z(d):
        return {"dp": y * nz + lax.rem(z + d + nz, nz)}

    def at_m(d):
        return {"mp": lax.rem(m + d, nm)}

    y_order, z_order, m_order = far_first(ny), far_first(nz), far_first(nm)

    barrier = pltpu.get_barrier_semaphore()
    peers = [at_y(d) for d in y_order] + [at_z(d) for d in z_order] + [at_m(d) for d in m_order]
    for peer in peers:
        pl.semaphore_signal(barrier, inc=1, device_id=peer, device_id_type=MESH)

    loads = []
    for place, (src, dst) in enumerate(
        ((hidden_hbm, hidden_ref), (down_hbm, down_ref), (up_hbm, up_ref))
    ):
        load = pltpu.make_async_copy(src, dst, load_sem.at[place])
        load.start()
        loads.append(load)

    def iota(shape, axis):
        return lax.broadcasted_iota(jnp.int32, shape, axis)

    def turned(row):
        n = row.shape[1]
        same = iota((n, n), 0) == iota((n, n), 1)
        return jnp.sum(jnp.where(same, row, 0.0), axis=1, keepdims=True)

    def place_of(owner, position):
        owner = owner.astype(jnp.int32)
        dy = lax.rem(lax.div(owner, nz) - y + ny, ny)
        dz = lax.rem(lax.rem(owner, nz) - z + nz, nz)
        flat = [offset for chunk in chunks for offset in chunk]
        z_slot = sum(jnp.where(dz == offset, i, 0) for i, offset in enumerate(flat))
        return (z_slot * ny + dy) * MOST + position.astype(jnp.int32)

    index_row = index_ref[...].astype(F32)
    slot_row = slot_ref[...].astype(F32)
    index_col, slot_col = turned(index_row), turned(slot_row)
    adapters = slot_row.shape[1]
    same = index_col == index_row
    row_at, col_at = iota((tokens, tokens), 0), iota((tokens, tokens), 1)
    position_row = jnp.sum(jnp.where(same & (row_at < col_at), 1.0, 0.0), axis=0, keepdims=True)
    position_col = jnp.sum(jnp.where(same & (col_at < row_at), 1.0, 0.0), axis=1, keepdims=True)
    named = iota((adapters, tokens), 0).astype(F32) == index_row
    owner_row = jnp.sum(jnp.where(named, slot_col, 0.0), axis=0, keepdims=True)
    named = iota((tokens, adapters), 1).astype(F32) == index_col
    owner_col = jnp.sum(jnp.where(named, slot_row, 0.0), axis=1, keepdims=True)
    target_row = place_of(owner_row, position_row)
    target_col = place_of(owner_col, position_col)

    groups = []

    def group(src_all, dst_all):
        made = Group(src_all, dst_all, send_sem.at[len(groups)], recv_sem.at[len(groups)])
        groups.append(made)
        return made

    def first_z(c):
        return 1 if chunks[c][0] == 0 else 0

    def y_copies(src, dst, c, sign):
        made = group(src.at[c, :, 1:ny], dst.at[c, :, 1:ny])
        made.start([(src.at[c, :, d], dst.at[c, :, d], at_y(sign * d)) for d in y_order])
        return made

    def z_copies(src, dst, c, sign):
        low = first_z(c)
        if low == nzc:
            return None
        made = group(src.at[c, low:nzc], dst.at[c, low:nzc])
        made.start(
            [(src.at[c, i], dst.at[c, i], at_z(sign * chunks[c][i])) for i in range(low, nzc)]
        )
        return made

    def received(made):
        if made is not None:
            made.wait_recv()

    def keep_y(src, dst, c):
        dst[c, :, 0] = src[c, :, 0]

    def keep_z(src, dst, c):
        if first_z(c):
            dst[c, 0] = src[c, 0]

    def pack(c):
        rows = lax.broadcasted_iota(jnp.int32, (slots, hidden_ref.shape[0]), 0) + c * slots
        pick = (rows == target_row).astype(F32).astype(BF16)
        packed = jnp.dot(pick, hidden_ref[...], preferred_element_type=F32).astype(BF16)
        pa[c] = packed[:, :half].reshape(nzc, ny, MOST, half)
        pb[c] = packed[:, half:].reshape(nzc, ny, MOST, half)

    def there_first(c):
        fa = y_copies(pa, qa, c, 1)
        fb = z_copies(pb, qb, c, 1)
        keep_y(pa, qa, c)
        keep_z(pb, qb, c)
        return fa, fb

    def there_second(c, first):
        fa, fb = first
        received(fa)
        second_a = z_copies(qa, ra, c, 1)
        received(fb)
        second_b = y_copies(qb, rb, c, 1)
        keep_z(qa, ra, c)
        keep_y(qb, rb, c)
        return second_a, second_b

    def rows_of(c, i):
        a = ra[c, i].reshape(ny * MOST, half)
        b = rb[c, i].reshape(ny * MOST, half)
        return jnp.concatenate([a, b], axis=1)

    def project(rows):
        down_part = lax.dot_general(rows, down_ref[...], NT, preferred_element_type=F32)
        up_part = lax.dot_general(rows, up_ref[...], NT, preferred_element_type=F32)
        return down_part, up_part[:, : cols - rank]

    def share(parts, landing):
        made = group(landing.at[1:nm], landing.at[1:nm])
        made.start([(parts.at[lax.rem(m + d, nm)], landing.at[d], at_m(d)) for d in m_order])
        return made

    def spread(held):
        made = group(held.at[1:nm], held.at[1:nm])
        made.start([(held.at[0], held.at[d], at_m(d)) for d in m_order])
        return made

    def total_of(parts, landing):
        total = parts[m]
        for d in range(1, nm):
            total += landing[d]
        return total

    def partials(c, second):
        for made in second:
            received(made)
        for i in range(nzc):
            rows = rows_of(c, i)
            down_part, up_part = project(rows)
            wide = rows.astype(F32)
            square = jnp.sum(wide * wide, axis=1, keepdims=True)
            whole = jnp.concatenate(
                [down_part, up_part, jnp.broadcast_to(square, (rows.shape[0], rank))], axis=1
            )
            per = zs.shape[2]
            count = rows.shape[0] // per
            zs[c, i * count : (i + 1) * count] = whole.reshape(count, per, 2 * cols)
        return share(zs.at[c], rz.at[c])

    def solve(c, shared):
        shared.wait_recv()
        total = total_of(zs.at[c], rz.at[c])
        square = total[:, 2 * cols - 1 :]
        lows = []
        extra = jnp.zeros_like(total)
        for layer in range(layers):
            term = total[:, layer * rank : (layer + 1) * rank]
            mean = square
            if layer > 0:
                term = term + extra[:, layer * rank : (layer + 1) * rank]
                known = layer * rank
                lean = 2.0 * total[:, cols : cols + known] + extra[:, cols : cols + known]
                mean = square + jnp.sum(
                    jnp.concatenate(lows, axis=1) * lean, axis=1, keepdims=True
                )
            scale = lax.rsqrt(jnp.maximum(mean, 0.0) * (1.0 / width) + EPSILON)
            low = (term * scale).astype(BF16)
            lw[c, 0, :, layer * rank : (layer + 1) * rank] = low
            lows.append(low.astype(F32))
            if layer < layers - 1:
                extra = extra + jnp.dot(
                    lows[-1],
                    gf[layer * rank : (layer + 1) * rank],
                    preferred_element_type=F32,
                    precision=lax.Precision.HIGHEST,
                )
        return spread(lw.at[c])

    def finish(c, told):
        told.wait_recv()
        count = nm // nzc
        for i in range(nzc):
            low = jnp.concatenate(
                [lw[c, lax.rem(m - (i * count + j) + nm, nm)] for j in range(count)], axis=0
            )
            update = jnp.dot(low, up_ref[...], preferred_element_type=F32)
            done = (rows_of(c, i).astype(F32) + update).astype(BF16)
            wa[c, i] = done[:, :half].reshape(ny, MOST, half)
            wb[c, i] = done[:, half:].reshape(ny, MOST, half)
        back_a = z_copies(wa, sa, c, -1)
        back_b = y_copies(wb, sb, c, -1)
        keep_z(wa, sa, c)
        keep_y(wb, sb, c)
        return back_a, back_b

    def back_second(c, first):
        back_a, back_b = first
        received(back_a)
        second_a = y_copies(sa, ta, c, -1)
        received(back_b)
        second_b = z_copies(sb, tb, c, -1)
        keep_y(sa, ta, c)
        keep_z(sb, tb, c)
        return second_a, second_b

    def unpack(c, second):
        for made in second:
            received(made)
        lanes = lax.broadcasted_iota(jnp.int32, (hidden_ref.shape[0], slots), 1) + c * slots
        pick = (lanes == target_col).astype(F32).astype(BF16)
        for h, t in ((0, ta), (1, tb)):
            part = jnp.dot(pick, t[c].reshape(slots, half), preferred_element_type=F32)
            cut = slice(h * half, (h + 1) * half)
            if c > 0:
                part = part + acc[:, cut]
            if c < nc - 1:
                acc[:, cut] = part
            else:
                out_ref[:, cut] = part.astype(BF16)

    def gram_parts():
        down_part, up_part = project(up_ref[: cols - rank])
        whole = jnp.concatenate(
            [down_part, up_part, jnp.zeros((cols - rank, rank), F32)], axis=1
        )
        gs[...] = whole.reshape(gs.shape)

    def gram_sum(shared):
        shared.wait_recv()
        ga[0] = total_of(gs, rg)
        return spread(ga)

    def gram_end(told):
        told.wait_recv()
        per = ga.shape[1]
        for j in range(nm):
            gf[j * per : (j + 1) * per] = ga[lax.rem(m - j + nm, nm)]

    loads[0].wait()
    for c in range(nc):
        pack(c)
    loads[1].wait()
    loads[2].wait()
    gram_parts()
    pl.semaphore_wait(barrier, len(peers))

    first, second, shared, told, back, last, gram = [{} for _ in range(7)]

    def do_first(c):
        first[c] = there_first(c)

    def do_second(c):
        second[c] = there_second(c, first[c])

    def do_gram_share(c):
        gram[0] = share(gs, rg)

    def do_gram_sum(c):
        gram[1] = gram_sum(gram[0])

    def do_gram_end(c):
        gram_end(gram[1])

    def do_partials(c):
        shared[c] = partials(c, second[c])

    def do_solve(c):
        told[c] = solve(c, shared[c])

    def do_finish(c):
        back[c] = finish(c, told[c])

    def do_back(c):
        last[c] = back_second(c, back[c])

    def do_unpack(c):
        unpack(c, last[c])

    steps = {
        "F": do_first,
        "G": do_second,
        "P": do_partials,
        "S": do_solve,
        "U": do_finish,
        "B": do_back,
        "O": do_unpack,
        "x": do_gram_share,
        "y": do_gram_sum,
        "z": do_gram_end,
    }
    for step in ORDER.split():
        c = int(step[1])
        if c < nc:
            steps[step[0]](c)
    for made in groups:
        made.wait_send()


def grid_of(n):
    side = 1
    while side * side < n:
        side *= 2
    return n // side, side


def local(hidden_state_rows, request_adapter_index, adapter_store_slot, down_weight_store, up_weight_store):
    tokens, width_dev = hidden_state_rows.shape
    ny, nz = grid_of(lax.axis_size("dp"))
    nm = lax.axis_size("mp")
    _, layers, _, rank = down_weight_store.shape
    cols = layers * rank
    chunks = chunks_of(nz)
    nc, nzc = len(chunks), len(chunks[0])
    half = width_dev // 2

    blocks = pltpu.VMEM((nc, nzc, ny, MOST, half), BF16)
    per = nzc * ny * MOST // nm
    gram_rows = (cols - rank) // nm
    n_groups = 10 * nc + 2
    return pl.pallas_call(
        functools.partial(kernel, ny, nz, nm, width_dev * nm, layers),
        out_shape=jax.ShapeDtypeStruct((tokens, width_dev), BF16),
        in_specs=[pl.BlockSpec(memory_space=pltpu.VMEM)] * 2
        + [pl.BlockSpec(memory_space=pl.ANY)] * 3,
        out_specs=pl.BlockSpec(memory_space=pltpu.VMEM),
        scratch_shapes=[
            pltpu.VMEM((tokens, width_dev), BF16),
            pltpu.VMEM((cols, width_dev), BF16),
            pltpu.VMEM((cols, width_dev), BF16),
            pltpu.SemaphoreType.DMA((3,)),
        ]
        + [blocks] * 12
        + [
            pltpu.VMEM((nc, nm, per, 2 * cols), F32),
            pltpu.VMEM((nc, nm, per, 2 * cols), F32),
            pltpu.VMEM((nc, nm, per, cols), BF16),
            pltpu.VMEM((nm, gram_rows, 2 * cols), F32),
            pltpu.VMEM((nm, gram_rows, 2 * cols), F32),
            pltpu.VMEM((nm, gram_rows, 2 * cols), F32),
            pltpu.VMEM((cols - rank, 2 * cols), F32),
            pltpu.VMEM((tokens, width_dev), F32),
            pltpu.SemaphoreType.DMA((n_groups,)),
            pltpu.SemaphoreType.DMA((n_groups,)),
        ],
        compiler_params=pltpu.CompilerParams(
            collective_id=0, has_side_effects=True, vmem_limit_bytes=60000 * 1024
        ),
    )(
        request_adapter_index[None, :],
        adapter_store_slot[None, :],
        hidden_state_rows,
        jnp.swapaxes(down_weight_store[0], 1, 2).reshape(cols, width_dev),
        up_weight_store[0].reshape(cols, width_dev),
    )


def solution(mesh):
    return jax.shard_map(
        local,
        mesh=mesh,
        in_specs=(
            P("dp", "mp"),
            P("dp"),
            P(),
            P("dp", None, "mp", None),
            P("dp", None, None, "mp"),
        ),
        out_specs=P("dp", "mp"),
        check_vma=False,
    )
```

```python
import functools

import jax
import jax.numpy as jnp
from jax import lax
from jax.experimental import pallas as pl
from jax.experimental.pallas import tpu as pltpu
from jax.sharding import PartitionSpec as P

MESH = pl.DeviceIdType.MESH
ORDER = (
    "F0", "F1", "x0", "G0", "F2", "y0", "G1", "F3",
    "z0", "P0", "G2", "S0", "P1", "U0", "G3", "S1",
    "P2", "B0", "U1", "P3", "S2", "B1", "U2", "S3",
    "O0", "U3", "B2", "O1", "B3", "O2", "O3",
)
F32 = jnp.float32
BF16 = jnp.bfloat16
EPSILON = 1e-05
MOST = 16
NT = (((1,), (1,)), ((), ()))


def far_first(n):
    order = []
    for step in range(n // 2, 0, -1):
        if n - step != step:
            order.append(n - step)
        order.append(step)
    return order


def chunks_of(nz):
    if nz == 8:
        return [[0, 4], [2, 6], [1, 7], [3, 5]]
    return [[dz] for dz in range(nz)]


class Group:
    def __init__(self, src_all, dst_all, send_sem, recv_sem):
        self.src_all, self.dst_all, self.send_sem, self.recv_sem = src_all, dst_all, send_sem, recv_sem

    def start(self, copies):
        for src, dst, device in copies:
            self.whole(src, dst, device).start()
        self.device = copies[0][2]

    def whole(self, src, dst, device):
        return pltpu.make_async_remote_copy(
            src_ref=src,
            dst_ref=dst,
            send_sem=self.send_sem,
            recv_sem=self.recv_sem,
            device_id=device,
            device_id_type=MESH,
        )

    def wait_recv(self):
        self.whole(self.dst_all, self.dst_all, self.device).wait_recv()

    def wait_send(self):
        self.whole(self.src_all, self.src_all, self.device).wait_send()


def kernel(
    ny,
    nz,
    nm,
    width,
    layers,
    index_ref,
    slot_ref,
    hidden_hbm,
    down_hbm,
    up_hbm,
    out_ref,
    hidden_ref,
    down_ref,
    up_ref,
    held_ref,
    load_sem,
    pa,
    pb,
    qa,
    qb,
    ra,
    rb,
    wa,
    wb,
    sa,
    sb,
    ta,
    tb,
    zs,
    rz,
    lw,
    gs,
    rg,
    ga,
    gf,
    acc,
    send_sem,
    recv_sem,
):
    chunks = chunks_of(nz)
    nc, nzc = len(chunks), len(chunks[0])
    cols = down_ref.shape[0]
    rank = cols // layers
    tokens = hidden_ref.shape[0]
    half = hidden_ref.shape[1] // 2
    slots = nzc * ny * MOST
    me = lax.axis_index("dp")
    m = lax.axis_index("mp")
    y, z = lax.div(me, nz), lax.rem(me, nz)

    def at_y(d):
        return {"dp": lax.rem(y + d + ny, ny) * nz + z}

    def at_z(d):
        return {"dp": y * nz + lax.rem(z + d + nz, nz)}

    def at_m(d):
        return {"mp": lax.rem(m + d, nm)}

    y_order, z_order, m_order = far_first(ny), far_first(nz), far_first(nm)

    barrier = pltpu.get_barrier_semaphore()
    peers = [at_y(d) for d in y_order] + [at_z(d) for d in z_order] + [at_m(d) for d in m_order]
    for peer in peers:
        pl.semaphore_signal(barrier, inc=1, device_id=peer, device_id_type=MESH)

    loads = []
    for place, (src, dst) in enumerate(
        ((hidden_hbm, hidden_ref), (down_hbm, down_ref), (up_hbm, up_ref))
    ):
        load = pltpu.make_async_copy(src, dst, load_sem.at[place])
        load.start()
        loads.append(load)

    def iota(shape, axis):
        return lax.broadcasted_iota(jnp.int32, shape, axis)

    def turned(row):
        n = row.shape[1]
        same = iota((n, n), 0) == iota((n, n), 1)
        return jnp.sum(jnp.where(same, row, 0.0), axis=1, keepdims=True)

    def place_of(owner, position):
        owner = owner.astype(jnp.int32)
        dy = lax.rem(lax.div(owner, nz) - y + ny, ny)
        dz = lax.rem(lax.rem(owner, nz) - z + nz, nz)
        flat = [offset for chunk in chunks for offset in chunk]
        z_slot = sum(jnp.where(dz == offset, i, 0) for i, offset in enumerate(flat))
        return (z_slot * ny + dy) * MOST + position.astype(jnp.int32)

    index_row = index_ref[...].astype(F32)
    slot_row = slot_ref[...].astype(F32)
    index_col, slot_col = turned(index_row), turned(slot_row)
    adapters = slot_row.shape[1]
    same = index_col == index_row
    row_at, col_at = iota((tokens, tokens), 0), iota((tokens, tokens), 1)
    position_row = jnp.sum(jnp.where(same & (row_at < col_at), 1.0, 0.0), axis=0, keepdims=True)
    position_col = jnp.sum(jnp.where(same & (col_at < row_at), 1.0, 0.0), axis=1, keepdims=True)
    named = iota((adapters, tokens), 0).astype(F32) == index_row
    owner_row = jnp.sum(jnp.where(named, slot_col, 0.0), axis=0, keepdims=True)
    named = iota((tokens, adapters), 1).astype(F32) == index_col
    owner_col = jnp.sum(jnp.where(named, slot_row, 0.0), axis=1, keepdims=True)
    target_row = place_of(owner_row, position_row)
    target_col = place_of(owner_col, position_col)

    groups = []

    def group(src_all, dst_all):
        made = Group(src_all, dst_all, send_sem.at[len(groups)], recv_sem.at[len(groups)])
        groups.append(made)
        return made

    def first_z(c):
        return 1 if chunks[c][0] == 0 else 0

    def y_copies(src, dst, c, sign):
        made = group(src.at[c, :, 1:ny], dst.at[c, :, 1:ny])
        made.start([(src.at[c, :, d], dst.at[c, :, d], at_y(sign * d)) for d in y_order])
        return made

    def z_copies(src, dst, c, sign):
        low = first_z(c)
        if low == nzc:
            return None
        made = group(src.at[c, low:nzc], dst.at[c, low:nzc])
        made.start(
            [(src.at[c, i], dst.at[c, i], at_z(sign * chunks[c][i])) for i in range(low, nzc)]
        )
        return made

    def received(made):
        if made is not None:
            made.wait_recv()

    def keep_y(src, dst, c):
        dst[c, :, 0] = src[c, :, 0]

    def keep_z(src, dst, c):
        if first_z(c):
            dst[c, 0] = src[c, 0]

    def pack(c):
        rows = lax.broadcasted_iota(jnp.int32, (slots, hidden_ref.shape[0]), 0) + c * slots
        pick = (rows == target_row).astype(F32).astype(BF16)
        packed = jnp.dot(pick, hidden_ref[...], preferred_element_type=F32).astype(BF16)
        pa[c] = packed[:, :half].reshape(nzc, ny, MOST, half)
        pb[c] = packed[:, half:].reshape(nzc, ny, MOST, half)

    def there_first(c):
        fa = y_copies(pa, qa, c, 1)
        fb = z_copies(pb, qb, c, 1)
        keep_y(pa, qa, c)
        keep_z(pb, qb, c)
        return fa, fb

    def there_second(c, first):
        fa, fb = first
        received(fa)
        second_a = z_copies(qa, ra, c, 1)
        received(fb)
        second_b = y_copies(qb, rb, c, 1)
        keep_z(qa, ra, c)
        keep_y(qb, rb, c)
        return second_a, second_b

    def rows_of(c, i):
        a = ra[c, i].reshape(ny * MOST, half)
        b = rb[c, i].reshape(ny * MOST, half)
        return jnp.concatenate([a, b], axis=1)

    def project(rows):
        down_part = lax.dot_general(rows, down_ref[...], NT, preferred_element_type=F32)
        up_part = lax.dot_general(rows, up_ref[...], NT, preferred_element_type=F32)
        return down_part, up_part[:, : cols - rank]

    def share(parts, landing):
        made = group(landing.at[1:nm], landing.at[1:nm])
        made.start([(parts.at[lax.rem(m + d, nm)], landing.at[d], at_m(d)) for d in m_order])
        return made

    def spread(held):
        made = group(held.at[1:nm], held.at[1:nm])
        made.start([(held.at[0], held.at[d], at_m(d)) for d in m_order])
        return made

    def total_of(parts, landing):
        total = parts[m]
        for d in range(1, nm):
            total += landing[d]
        return total

    def partials(c, second):
        for made in second:
            received(made)
        for i in range(nzc):
            rows = rows_of(c, i)
            down_part, up_part = project(rows)
            wide = rows.astype(F32)
            square = jnp.sum(wide * wide, axis=1, keepdims=True)
            whole = jnp.concatenate(
                [down_part, up_part, jnp.broadcast_to(square, (rows.shape[0], rank))], axis=1
            )
            per = zs.shape[2]
            count = rows.shape[0] // per
            zs[c, i * count : (i + 1) * count] = whole.reshape(count, per, 2 * cols)
        return share(zs.at[c], rz.at[c])

    def solve(c, shared):
        shared.wait_recv()
        total = total_of(zs.at[c], rz.at[c])
        square = total[:, 2 * cols - 1 :]
        lows = []
        extra = jnp.zeros_like(total)
        for layer in range(layers):
            term = total[:, layer * rank : (layer + 1) * rank]
            mean = square
            if layer > 0:
                term = term + extra[:, layer * rank : (layer + 1) * rank]
                known = layer * rank
                lean = 2.0 * total[:, cols : cols + known] + extra[:, cols : cols + known]
                mean = square + jnp.sum(
                    jnp.concatenate(lows, axis=1) * lean, axis=1, keepdims=True
                )
            scale = lax.rsqrt(jnp.maximum(mean, 0.0) * (1.0 / width) + EPSILON)
            low = (term * scale).astype(BF16)
            lw[c, 0, :, layer * rank : (layer + 1) * rank] = low
            lows.append(low.astype(F32))
            if layer < layers - 1:
                extra = extra + jnp.dot(
                    lows[-1],
                    gf[layer * rank : (layer + 1) * rank],
                    preferred_element_type=F32,
                    precision=lax.Precision.HIGHEST,
                )
        return spread(lw.at[c])

    def finish(c, told):
        told.wait_recv()
        count = nm // nzc
        for i in range(nzc):
            low = jnp.concatenate(
                [lw[c, lax.rem(m - (i * count + j) + nm, nm)] for j in range(count)], axis=0
            )
            update = jnp.dot(low, up_ref[...], preferred_element_type=F32)
            done = (rows_of(c, i).astype(F32) + update).astype(BF16)
            wa[c, i] = done[:, :half].reshape(ny, MOST, half)
            wb[c, i] = done[:, half:].reshape(ny, MOST, half)
        back_a = z_copies(wa, sa, c, -1)
        back_b = y_copies(wb, sb, c, -1)
        keep_z(wa, sa, c)
        keep_y(wb, sb, c)
        return back_a, back_b

    def back_second(c, first):
        back_a, back_b = first
        received(back_a)
        second_a = y_copies(sa, ta, c, -1)
        received(back_b)
        second_b = z_copies(sb, tb, c, -1)
        keep_y(sa, ta, c)
        keep_z(sb, tb, c)
        return second_a, second_b

    def unpack(c, second):
        lanes = lax.broadcasted_iota(jnp.int32, (hidden_ref.shape[0], slots), 1) + c * slots
        pick = (lanes == target_col).astype(F32).astype(BF16)
        for h, t in ((0, ta), (1, tb)):
            received(second[h])
            part = jnp.dot(pick, t[c].reshape(slots, half), preferred_element_type=F32)
            cut = slice(h * half, (h + 1) * half)
            if c > 0:
                part = part + acc[:, cut]
            if c < nc - 1:
                acc[:, cut] = part
            else:
                held_ref[:, cut] = part.astype(BF16)
                copy = pltpu.make_async_copy(
                    held_ref.at[:, cut], out_ref.at[:, cut], load_sem.at[3 + h]
                )
                copy.start()
                loads.append(copy)

    def gram_parts():
        down_part, up_part = project(up_ref[: cols - rank])
        whole = jnp.concatenate(
            [down_part, up_part, jnp.zeros((cols - rank, rank), F32)], axis=1
        )
        gs[...] = whole.reshape(gs.shape)

    def gram_sum(shared):
        shared.wait_recv()
        ga[0] = total_of(gs, rg)
        return spread(ga)

    def gram_end(told):
        told.wait_recv()
        per = ga.shape[1]
        for j in range(nm):
            gf[j * per : (j + 1) * per] = ga[lax.rem(m - j + nm, nm)]

    loads[0].wait()
    for c in range(nc):
        pack(c)
    loads[1].wait()
    loads[2].wait()
    gram_parts()
    pl.semaphore_wait(barrier, len(peers))

    first, second, shared, told, back, last, gram = [{} for _ in range(7)]

    def do_first(c):
        first[c] = there_first(c)

    def do_second(c):
        second[c] = there_second(c, first[c])

    def do_gram_share(c):
        gram[0] = share(gs, rg)

    def do_gram_sum(c):
        gram[1] = gram_sum(gram[0])

    def do_gram_end(c):
        gram_end(gram[1])

    def do_partials(c):
        shared[c] = partials(c, second[c])

    def do_solve(c):
        told[c] = solve(c, shared[c])

    def do_finish(c):
        back[c] = finish(c, told[c])

    def do_back(c):
        last[c] = back_second(c, back[c])

    def do_unpack(c):
        unpack(c, last[c])

    steps = {
        "F": do_first,
        "G": do_second,
        "P": do_partials,
        "S": do_solve,
        "U": do_finish,
        "B": do_back,
        "O": do_unpack,
        "x": do_gram_share,
        "y": do_gram_sum,
        "z": do_gram_end,
    }
    for step in ORDER:
        c = int(step[1])
        if c < nc:
            steps[step[0]](c)
    for made in groups:
        made.wait_send()
    for copy in loads[3:]:
        copy.wait()


def grid_of(n):
    side = 1
    while side * side < n:
        side *= 2
    return n // side, side


def local(hidden_state_rows, request_adapter_index, adapter_store_slot, down_weight_store, up_weight_store):
    tokens, width_dev = hidden_state_rows.shape
    ny, nz = grid_of(lax.axis_size("dp"))
    nm = lax.axis_size("mp")
    _, layers, _, rank = down_weight_store.shape
    cols = layers * rank
    chunks = chunks_of(nz)
    nc, nzc = len(chunks), len(chunks[0])
    half = width_dev // 2

    blocks = pltpu.VMEM((nc, nzc, ny, MOST, half), BF16)
    per = nzc * ny * MOST // nm
    gram_rows = (cols - rank) // nm
    n_groups = 10 * nc + 2
    return pl.pallas_call(
        functools.partial(kernel, ny, nz, nm, width_dev * nm, layers),
        out_shape=jax.ShapeDtypeStruct((tokens, width_dev), BF16),
        in_specs=[pl.BlockSpec(memory_space=pltpu.VMEM)] * 2
        + [pl.BlockSpec(memory_space=pl.ANY)] * 3,
        out_specs=pl.BlockSpec(memory_space=pl.ANY),
        scratch_shapes=[
            pltpu.VMEM((tokens, width_dev), BF16),
            pltpu.VMEM((cols, width_dev), BF16),
            pltpu.VMEM((cols, width_dev), BF16),
            pltpu.VMEM((tokens, width_dev), BF16),
            pltpu.SemaphoreType.DMA((5,)),
        ]
        + [blocks] * 12
        + [
            pltpu.VMEM((nc, nm, per, 2 * cols), F32),
            pltpu.VMEM((nc, nm, per, 2 * cols), F32),
            pltpu.VMEM((nc, nm, per, cols), BF16),
            pltpu.VMEM((nm, gram_rows, 2 * cols), F32),
            pltpu.VMEM((nm, gram_rows, 2 * cols), F32),
            pltpu.VMEM((nm, gram_rows, 2 * cols), F32),
            pltpu.VMEM((cols - rank, 2 * cols), F32),
            pltpu.VMEM((tokens, width_dev), F32),
            pltpu.SemaphoreType.DMA((n_groups,)),
            pltpu.SemaphoreType.DMA((n_groups,)),
        ],
        compiler_params=pltpu.CompilerParams(
            collective_id=0, has_side_effects=True, vmem_limit_bytes=60000 * 1024
        ),
    )(
        request_adapter_index[None, :],
        adapter_store_slot[None, :],
        hidden_state_rows,
        jnp.swapaxes(down_weight_store[0], 1, 2).reshape(cols, width_dev),
        up_weight_store[0].reshape(cols, width_dev),
    )


def solution(mesh):
    return jax.shard_map(
        local,
        mesh=mesh,
        in_specs=(
            P("dp", "mp"),
            P("dp"),
            P(),
            P("dp", None, "mp", None),
            P("dp", None, None, "mp"),
        ),
        out_specs=P("dp", "mp"),
        check_vma=False,
    )
```

```python
import functools

import jax
import jax.numpy as jnp
from jax import lax
from jax.experimental import pallas as pl
from jax.experimental.pallas import tpu as pltpu
from jax.sharding import PartitionSpec as P

MESH = pl.DeviceIdType.MESH
ORDER = (
    "F0", "F1", "x0", "G0", "F2", "y0", "G1", "F3",
    "z0", "P0", "G2", "S0", "P1", "U0", "G3", "S1",
    "P2", "B0", "U1", "P3", "S2", "B1", "U2", "S3",
    "U3", "B2", "O0", "O1", "B3", "O2", "O3",
)
F32 = jnp.float32
BF16 = jnp.bfloat16
EPSILON = 1e-05
MOST = 16
NT = (((1,), (1,)), ((), ()))


def far_first(n):
    order = []
    for step in range(n // 2, 0, -1):
        if n - step != step:
            order.append(n - step)
        order.append(step)
    return order


def chunks_of(nz):
    if nz == 8:
        return [[0, 4], [2, 6], [1, 7], [3, 5]]
    return [[dz] for dz in range(nz)]


class Group:
    def __init__(self, src_all, dst_all, send_sem, recv_sem):
        self.src_all, self.dst_all, self.send_sem, self.recv_sem = src_all, dst_all, send_sem, recv_sem

    def start(self, copies):
        for src, dst, device in copies:
            self.whole(src, dst, device).start()
        self.device = copies[0][2]

    def whole(self, src, dst, device):
        return pltpu.make_async_remote_copy(
            src_ref=src,
            dst_ref=dst,
            send_sem=self.send_sem,
            recv_sem=self.recv_sem,
            device_id=device,
            device_id_type=MESH,
        )

    def wait_recv(self):
        self.whole(self.dst_all, self.dst_all, self.device).wait_recv()

    def wait_send(self):
        self.whole(self.src_all, self.src_all, self.device).wait_send()


def kernel(
    ny,
    nz,
    nm,
    width,
    layers,
    index_ref,
    slot_ref,
    hidden_hbm,
    down_hbm,
    up_hbm,
    out_ref,
    hidden_ref,
    down_ref,
    up_ref,
    held_ref,
    load_sem,
    pa,
    pb,
    qa,
    qb,
    ra,
    rb,
    wa,
    wb,
    sa,
    sb,
    ta,
    tb,
    zs,
    rz,
    lw,
    gs,
    rg,
    ga,
    gf,
    acc,
    send_sem,
    recv_sem,
):
    chunks = chunks_of(nz)
    nc, nzc = len(chunks), len(chunks[0])
    cols = down_ref.shape[0]
    rank = cols // layers
    tokens = hidden_ref.shape[0]
    half = hidden_ref.shape[1] // 2
    slots = nzc * ny * MOST
    me = lax.axis_index("dp")
    m = lax.axis_index("mp")
    y, z = lax.div(me, nz), lax.rem(me, nz)

    def at_y(d):
        return {"dp": lax.rem(y + d + ny, ny) * nz + z}

    def at_z(d):
        return {"dp": y * nz + lax.rem(z + d + nz, nz)}

    def at_m(d):
        return {"mp": lax.rem(m + d, nm)}

    y_order, z_order, m_order = far_first(ny), far_first(nz), far_first(nm)

    barrier = pltpu.get_barrier_semaphore()
    peers = [at_y(d) for d in y_order] + [at_z(d) for d in z_order] + [at_m(d) for d in m_order]
    for peer in peers:
        pl.semaphore_signal(barrier, inc=1, device_id=peer, device_id_type=MESH)

    loads = []
    for place, (src, dst) in enumerate(
        ((hidden_hbm, hidden_ref), (down_hbm, down_ref), (up_hbm, up_ref))
    ):
        load = pltpu.make_async_copy(src, dst, load_sem.at[place])
        load.start()
        loads.append(load)

    def iota(shape, axis):
        return lax.broadcasted_iota(jnp.int32, shape, axis)

    def turned(row):
        n = row.shape[1]
        same = iota((n, n), 0) == iota((n, n), 1)
        return jnp.sum(jnp.where(same, row, 0.0), axis=1, keepdims=True)

    def place_of(owner, position):
        owner = owner.astype(jnp.int32)
        dy = lax.rem(lax.div(owner, nz) - y + ny, ny)
        dz = lax.rem(lax.rem(owner, nz) - z + nz, nz)
        flat = [offset for chunk in chunks for offset in chunk]
        z_slot = sum(jnp.where(dz == offset, i, 0) for i, offset in enumerate(flat))
        return (z_slot * ny + dy) * MOST + position.astype(jnp.int32)

    index_row = index_ref[...].astype(F32)
    slot_row = slot_ref[...].astype(F32)
    index_col, slot_col = turned(index_row), turned(slot_row)
    adapters = slot_row.shape[1]
    same = index_col == index_row
    row_at, col_at = iota((tokens, tokens), 0), iota((tokens, tokens), 1)
    position_row = jnp.sum(jnp.where(same & (row_at < col_at), 1.0, 0.0), axis=0, keepdims=True)
    position_col = jnp.sum(jnp.where(same & (col_at < row_at), 1.0, 0.0), axis=1, keepdims=True)
    named = iota((adapters, tokens), 0).astype(F32) == index_row
    owner_row = jnp.sum(jnp.where(named, slot_col, 0.0), axis=0, keepdims=True)
    named = iota((tokens, adapters), 1).astype(F32) == index_col
    owner_col = jnp.sum(jnp.where(named, slot_row, 0.0), axis=1, keepdims=True)
    target_row = place_of(owner_row, position_row)
    target_col = place_of(owner_col, position_col)

    groups = []

    def group(src_all, dst_all):
        made = Group(src_all, dst_all, send_sem.at[len(groups)], recv_sem.at[len(groups)])
        groups.append(made)
        return made

    def first_z(c):
        return 1 if chunks[c][0] == 0 else 0

    def y_copies(src, dst, c, sign):
        made = group(src.at[c, :, 1:ny], dst.at[c, :, 1:ny])
        made.start([(src.at[c, :, d], dst.at[c, :, d], at_y(sign * d)) for d in y_order])
        return made

    def z_copies(src, dst, c, sign):
        low = first_z(c)
        if low == nzc:
            return None
        made = group(src.at[c, low:nzc], dst.at[c, low:nzc])
        made.start(
            [(src.at[c, i], dst.at[c, i], at_z(sign * chunks[c][i])) for i in range(low, nzc)]
        )
        return made

    def received(made):
        if made is not None:
            made.wait_recv()

    def keep_y(src, dst, c):
        dst[c, :, 0] = src[c, :, 0]

    def keep_z(src, dst, c):
        if first_z(c):
            dst[c, 0] = src[c, 0]

    def pack(c):
        rows = lax.broadcasted_iota(jnp.int32, (slots, hidden_ref.shape[0]), 0) + c * slots
        pick = (rows == target_row).astype(F32).astype(BF16)
        packed = jnp.dot(pick, hidden_ref[...], preferred_element_type=F32).astype(BF16)
        pa[c] = packed[:, :half].reshape(nzc, ny, MOST, half)
        pb[c] = packed[:, half:].reshape(nzc, ny, MOST, half)

    def there_first(c):
        fa = y_copies(pa, qa, c, 1)
        fb = z_copies(pb, qb, c, 1)
        keep_y(pa, qa, c)
        keep_z(pb, qb, c)
        return fa, fb

    def there_second(c, first):
        fa, fb = first
        received(fa)
        second_a = z_copies(qa, ra, c, 1)
        received(fb)
        second_b = y_copies(qb, rb, c, 1)
        keep_z(qa, ra, c)
        keep_y(qb, rb, c)
        return second_a, second_b

    def rows_of(c, i):
        a = ra[c, i].reshape(ny * MOST, half)
        b = rb[c, i].reshape(ny * MOST, half)
        return jnp.concatenate([a, b], axis=1)

    def project(rows):
        down_part = lax.dot_general(rows, down_ref[...], NT, preferred_element_type=F32)
        up_part = lax.dot_general(rows, up_ref[...], NT, preferred_element_type=F32)
        return down_part, up_part[:, : cols - rank]

    def share(parts, landing):
        made = group(landing.at[1:nm], landing.at[1:nm])
        made.start([(parts.at[lax.rem(m + d, nm)], landing.at[d], at_m(d)) for d in m_order])
        return made

    def spread(held):
        made = group(held.at[1:nm], held.at[1:nm])
        made.start([(held.at[0], held.at[d], at_m(d)) for d in m_order])
        return made

    def total_of(parts, landing):
        total = parts[m]
        for d in range(1, nm):
            total += landing[d]
        return total

    def partials(c, second):
        for made in second:
            received(made)
        for i in range(nzc):
            rows = rows_of(c, i)
            down_part, up_part = project(rows)
            wide = rows.astype(F32)
            square = jnp.sum(wide * wide, axis=1, keepdims=True)
            whole = jnp.concatenate(
                [down_part, up_part, jnp.broadcast_to(square, (rows.shape[0], rank))], axis=1
            )
            per = zs.shape[2]
            count = rows.shape[0] // per
            zs[c, i * count : (i + 1) * count] = whole.reshape(count, per, 2 * cols)
        return share(zs.at[c], rz.at[c])

    def solve(c, shared):
        shared.wait_recv()
        total = total_of(zs.at[c], rz.at[c])
        square = total[:, 2 * cols - 1 :]
        lows = []
        extra = jnp.zeros_like(total)
        for layer in range(layers):
            term = total[:, layer * rank : (layer + 1) * rank]
            mean = square
            if layer > 0:
                term = term + extra[:, layer * rank : (layer + 1) * rank]
                known = layer * rank
                lean = 2.0 * total[:, cols : cols + known] + extra[:, cols : cols + known]
                mean = square + jnp.sum(
                    jnp.concatenate(lows, axis=1) * lean, axis=1, keepdims=True
                )
            scale = lax.rsqrt(jnp.maximum(mean, 0.0) * (1.0 / width) + EPSILON)
            low = (term * scale).astype(BF16)
            lw[c, 0, :, layer * rank : (layer + 1) * rank] = low
            lows.append(low.astype(F32))
            if layer < layers - 1:
                extra = extra + jnp.dot(
                    lows[-1],
                    gf[layer * rank : (layer + 1) * rank],
                    preferred_element_type=F32,
                    precision=lax.Precision.HIGHEST,
                )
        return spread(lw.at[c])

    def finish(c, told):
        told.wait_recv()
        count = nm // nzc
        for i in range(nzc):
            low = jnp.concatenate(
                [lw[c, lax.rem(m - (i * count + j) + nm, nm)] for j in range(count)], axis=0
            )
            update = jnp.dot(low, up_ref[...], preferred_element_type=F32)
            done = (rows_of(c, i).astype(F32) + update).astype(BF16)
            wa[c, i] = done[:, :half].reshape(ny, MOST, half)
            wb[c, i] = done[:, half:].reshape(ny, MOST, half)
        back_a = z_copies(wa, sa, c, -1)
        back_b = y_copies(wb, sb, c, -1)
        keep_z(wa, sa, c)
        keep_y(wb, sb, c)
        return back_a, back_b

    def back_second(c, first):
        back_a, back_b = first
        received(back_a)
        second_a = y_copies(sa, ta, c, -1)
        received(back_b)
        second_b = z_copies(sb, tb, c, -1)
        keep_y(sa, ta, c)
        keep_z(sb, tb, c)
        return second_a, second_b

    def unpack(c, second):
        lanes = lax.broadcasted_iota(jnp.int32, (hidden_ref.shape[0], slots), 1) + c * slots
        pick = (lanes == target_col).astype(F32).astype(BF16)
        for h, t in ((0, ta), (1, tb)):
            received(second[h])
            part = jnp.dot(pick, t[c].reshape(slots, half), preferred_element_type=F32)
            cut = slice(h * half, (h + 1) * half)
            if c > 0:
                part = part + acc[:, cut]
            if c < nc - 1:
                acc[:, cut] = part
            else:
                held_ref[:, cut] = part.astype(BF16)
                copy = pltpu.make_async_copy(
                    held_ref.at[:, cut], out_ref.at[:, cut], load_sem.at[3 + h]
                )
                copy.start()
                loads.append(copy)

    def gram_parts():
        down_part, up_part = project(up_ref[: cols - rank])
        whole = jnp.concatenate(
            [down_part, up_part, jnp.zeros((cols - rank, rank), F32)], axis=1
        )
        gs[...] = whole.reshape(gs.shape)

    def gram_sum(shared):
        shared.wait_recv()
        ga[0] = total_of(gs, rg)
        return spread(ga)

    def gram_end(told):
        told.wait_recv()
        per = ga.shape[1]
        for j in range(nm):
            gf[j * per : (j + 1) * per] = ga[lax.rem(m - j + nm, nm)]

    loads[0].wait()
    for c in range(nc):
        pack(c)
    loads[1].wait()
    loads[2].wait()
    gram_parts()
    pl.semaphore_wait(barrier, len(peers))

    first, second, shared, told, back, last, gram = [{} for _ in range(7)]

    def do_first(c):
        first[c] = there_first(c)

    def do_second(c):
        second[c] = there_second(c, first[c])

    def do_gram_share(c):
        gram[0] = share(gs, rg)

    def do_gram_sum(c):
        gram[1] = gram_sum(gram[0])

    def do_gram_end(c):
        gram_end(gram[1])

    def do_partials(c):
        shared[c] = partials(c, second[c])

    def do_solve(c):
        told[c] = solve(c, shared[c])

    def do_finish(c):
        back[c] = finish(c, told[c])

    def do_back(c):
        last[c] = back_second(c, back[c])

    def do_unpack(c):
        unpack(c, last[c])

    steps = {
        "F": do_first,
        "G": do_second,
        "P": do_partials,
        "S": do_solve,
        "U": do_finish,
        "B": do_back,
        "O": do_unpack,
        "x": do_gram_share,
        "y": do_gram_sum,
        "z": do_gram_end,
    }
    for step in ORDER:
        c = int(step[1])
        if c < nc:
            steps[step[0]](c)
    for made in groups:
        made.wait_send()
    for copy in loads[3:]:
        copy.wait()


def grid_of(n):
    side = 1
    while side * side < n:
        side *= 2
    return n // side, side


def local(hidden_state_rows, request_adapter_index, adapter_store_slot, down_weight_store, up_weight_store):
    tokens, width_dev = hidden_state_rows.shape
    ny, nz = grid_of(lax.axis_size("dp"))
    nm = lax.axis_size("mp")
    _, layers, _, rank = down_weight_store.shape
    cols = layers * rank
    chunks = chunks_of(nz)
    nc, nzc = len(chunks), len(chunks[0])
    half = width_dev // 2

    blocks = pltpu.VMEM((nc, nzc, ny, MOST, half), BF16)
    per = nzc * ny * MOST // nm
    gram_rows = (cols - rank) // nm
    n_groups = 10 * nc + 2
    return pl.pallas_call(
        functools.partial(kernel, ny, nz, nm, width_dev * nm, layers),
        out_shape=jax.ShapeDtypeStruct((tokens, width_dev), BF16),
        in_specs=[pl.BlockSpec(memory_space=pltpu.VMEM)] * 2
        + [pl.BlockSpec(memory_space=pl.ANY)] * 3,
        out_specs=pl.BlockSpec(memory_space=pl.ANY),
        scratch_shapes=[
            pltpu.VMEM((tokens, width_dev), BF16),
            pltpu.VMEM((cols, width_dev), BF16),
            pltpu.VMEM((cols, width_dev), BF16),
            pltpu.VMEM((tokens, width_dev), BF16),
            pltpu.SemaphoreType.DMA((5,)),
        ]
        + [blocks] * 12
        + [
            pltpu.VMEM((nc, nm, per, 2 * cols), F32),
            pltpu.VMEM((nc, nm, per, 2 * cols), F32),
            pltpu.VMEM((nc, nm, per, cols), BF16),
            pltpu.VMEM((nm, gram_rows, 2 * cols), F32),
            pltpu.VMEM((nm, gram_rows, 2 * cols), F32),
            pltpu.VMEM((nm, gram_rows, 2 * cols), F32),
            pltpu.VMEM((cols - rank, 2 * cols), F32),
            pltpu.VMEM((tokens, width_dev), F32),
            pltpu.SemaphoreType.DMA((n_groups,)),
            pltpu.SemaphoreType.DMA((n_groups,)),
        ],
        compiler_params=pltpu.CompilerParams(
            collective_id=0, has_side_effects=True, vmem_limit_bytes=60000 * 1024
        ),
    )(
        request_adapter_index[None, :],
        adapter_store_slot[None, :],
        hidden_state_rows,
        jnp.swapaxes(down_weight_store[0], 1, 2).reshape(cols, width_dev),
        up_weight_store[0].reshape(cols, width_dev),
    )


def solution(mesh):
    return jax.shard_map(
        local,
        mesh=mesh,
        in_specs=(
            P("dp", "mp"),
            P("dp"),
            P(),
            P("dp", None, "mp", None),
            P("dp", None, None, "mp"),
        ),
        out_specs=P("dp", "mp"),
        check_vma=False,
    )
```
